32 devices in a mesh: grp: 4 (over y, x), blk: 8 (over z, core).
Axes of the slice: x: 2, y: 2, z: 4, core: 2. Of those that a mesh axis runs over, the one named last changes fastest.
Arguments:
- features: float32 [32768, 128], P(('grp', 'blk')), may hold values from -6 to 6
- new_slot: int32 [256], P(('grp', 'blk')), may hold values from 0 to 255, as said below
- tile_values: float32 [4, 8, 8, 16, 128, 128], P('grp', 'blk'), may hold values from 0 to 0.04
- tile_dest: int32 [4, 8, 8, 16], P('grp', 'blk'), may hold values from -1 to 31, as said below
- tile_source: int32 [4, 8, 8, 16], P('grp', 'blk'), may hold values from -1 to 7, as said below
- weight: float32 [128, 128], replicated, may hold values from -0.5 to 0.5
- bias_vector: float32 [128], replicated, may hold values from -3 to 3
Outputs:
- activations: float32 [32768, 128], P(('grp', 'blk'))
The draws below stay inside these ranges and needn't reach their ends.
Inputs may be any that keep to these rules, and one draw needn't show every extreme that they name: new_slot is a permutation of the block positions that keeps every block in its range of 64 blocks; the 8 blocks of one device go to at most 8 - 1 devices of its range, at most 2 to any one device, a count that some device reaches; every device's new positions receive exactly 8 blocks. tile_dest[g, b, k, t] is -1 exactly where the slot is empty; the live slots of each (g, b, k) come first, from 1 to 16 of them, and every (g, b) has some k with all 16 live. tile_source is -1 exactly where tile_dest is -1.
All inputs are finite; a program needn't handle non-finite values.
Results may differ from the reference program's by a relative error of at most 0.0003.
Values sent between devices are 32-bit elements; how exact they have to be, the bound alone decides.
A program may use at most 128 MiB of HBM per device.

```python
import jax
import jax.numpy as jnp
from jax import lax

TILE = 128
FEAT = 128
BLOCKS_DEV = 8
TILE_SLOTS = 16
NODES = 32768
N_GRP = 4
N_BLK = 8


def draw_new_slot(key, part):
    cycle_count = N_BLK
    per_device = BLOCKS_DEV
    runs = cycle_count - 1
    sizes = per_device // runs + (jnp.arange(runs) < per_device % runs).astype(jnp.int32)
    ends = jnp.cumsum(sizes)
    order_ids = jnp.arange(per_device)
    run_of = jnp.sum((ends[None, :] <= order_ids[:, None]).astype(jnp.int32), axis=1)

    def one_group(group_key):
        first_key, second_key, third_key, fourth_key = jax.random.split(group_key, 4)
        offsets = jax.random.permutation(first_key, cycle_count)[:runs]
        rotate = jax.random.permutation(second_key, cycle_count)
        relabel = jax.random.permutation(third_key, cycle_count)
        scores = jax.random.randint(fourth_key, (cycle_count, per_device), 0, 1 << 20) * per_device + order_ids[None, :]
        within = jnp.argsort(scores, axis=1)
        target = relabel[(rotate[:, None] + offsets[run_of][None, :]) % cycle_count]
        landing = within[target, order_ids[None, :]]
        return target * per_device + landing
    tables = jax.vmap(one_group)(jax.random.split(jax.random.fold_in(key, 311), N_GRP))
    base = (jnp.arange(N_GRP) * (N_BLK * BLOCKS_DEV))[:, None, None]
    return (tables + base).reshape(-1).astype(jnp.int32)


def tile_layout(key):
    layout_key = jax.random.fold_in(key, 4242)
    first_key, second_key, third_key, fourth_key = jax.random.split(layout_key, 4)
    shape = (N_GRP, N_BLK, N_BLK)
    counts = jax.random.randint(first_key, shape, 1, TILE_SLOTS + 1)
    full_bucket = jax.random.randint(second_key, (N_GRP, N_BLK), 0, N_BLK)
    counts = jnp.where(jnp.arange(N_BLK)[None, None, :] == full_bucket[:, :, None], TILE_SLOTS, counts)
    live_slots = jnp.arange(TILE_SLOTS)[None, None, None, :] < counts[:, :, :, None]
    targets = jax.random.randint(third_key, shape + (TILE_SLOTS,), 0, N_GRP * BLOCKS_DEV)
    anchors = jax.random.randint(fourth_key, shape + (TILE_SLOTS,), 0, BLOCKS_DEV)
    return (jnp.where(live_slots, targets, -1).astype(jnp.int32), jnp.where(live_slots, anchors, -1).astype(jnp.int32))


def draw_tile_dest(key, part):
    return tile_layout(key)[0]


def draw_tile_source(key, part):
    return tile_layout(key)[1]


def level_of(stream_key, shape, cuts, smallest, high):
    loudness, own = 1.0, jax.random.fold_in(stream_key, 6)
    for dim, shards_of in cuts:
        steps = jnp.exp(jax.random.uniform(jax.random.fold_in(own, dim), (shards_of,), jnp.float32, smallest / len(cuts), high / len(cuts)))
        loudness = loudness * jnp.repeat(steps, shape[dim] // shards_of).reshape([-1 if axis == dim else 1 for axis in range(len(shape))])
    return loudness


def scatter_about(rng, dims, spread, reach, pieces=(), kind=jnp.bfloat16):
    values = spread * jax.random.normal(rng, dims, jnp.float32)
    if pieces:
        values = values * level_of(rng, dims, pieces, -0.22, 0.18)
    return jnp.clip(values, -reach, reach).astype(kind)


def setup_inputs(seed: int = 0) -> dict:
    seeds = jax.random.split(jax.random.key(seed), 8)
    features = scatter_about(seeds[0], (NODES, FEAT), 1.0, 6.0, ((0, 32),), jnp.float32)
    new_slot = draw_new_slot(jax.random.fold_in(seeds[7], 71), 0)
    tile_values = jnp.clip(0.04 * jax.random.uniform(seeds[2], (N_GRP, N_BLK, N_BLK, TILE_SLOTS, TILE, TILE), jnp.float32) ** level_of(seeds[2], (N_GRP, N_BLK, N_BLK, TILE_SLOTS, TILE, TILE), ((0, 4), (1, 8)), -0.2, 0.2), 0.0, 0.04)
    tile_dest = draw_tile_dest(jax.random.fold_in(seeds[7], 71), 0)
    tile_source = draw_tile_source(jax.random.fold_in(seeds[7], 71), 0)
    weight = scatter_about(seeds[5], (FEAT, FEAT), FEAT ** -0.5, 0.5, (), jnp.float32)
    bias_vector = scatter_about(seeds[6], (FEAT,), 0.5, 3.0, (), jnp.float32)
    return dict(features=features, new_slot=new_slot, tile_values=tile_values, tile_dest=tile_dest, tile_source=tile_source, weight=weight, bias_vector=bias_vector)


precise = lax.Precision.HIGHEST


def reference(features, new_slot, tile_values, tile_dest, tile_source, weight, bias_vector):
    range_blocks = N_BLK * BLOCKS_DEV
    all_blocks = N_GRP * range_blocks
    blocks = features.reshape(all_blocks, TILE, FEAT)
    reordered = jnp.zeros_like(blocks).at[new_slot.astype(jnp.int32)].set(blocks)
    devices_all = N_GRP * N_BLK
    device_ids = jnp.arange(devices_all, dtype=jnp.int32)
    group_ids = device_ids // N_BLK
    member_ids = device_ids % N_BLK
    bucket_ids = jnp.arange(N_BLK, dtype=jnp.int32)[:, None]

    def one_device(running, device_item):
        values, targets, anchors, group_id, member_id = device_item
        source_index = (group_id * range_blocks + bucket_ids * BLOCKS_DEV + jnp.maximum(anchors, 0)).astype(jnp.int32)
        clamped = jnp.maximum(targets, 0)
        dest_index = ((clamped // BLOCKS_DEV) * range_blocks + member_id * BLOCKS_DEV + clamped % BLOCKS_DEV).astype(jnp.int32)
        picked = reordered[source_index.reshape(-1)]
        products = jnp.einsum("ntr,nrf->ntf", values.reshape(-1, TILE, TILE).astype(jnp.float32), picked.astype(jnp.float32), precision=precise)
        live_mask = (targets >= 0).astype(jnp.float32).reshape(-1, 1, 1)
        return running.at[dest_index.reshape(-1)].add(products * live_mask), None

    start_sum = jnp.zeros((all_blocks, TILE, FEAT), jnp.float32)
    aggregated, unused = lax.scan(
        one_device,
        start_sum,
        (
            tile_values.reshape(devices_all, N_BLK, TILE_SLOTS, TILE, TILE),
            tile_dest.reshape(devices_all, N_BLK, TILE_SLOTS),
            tile_source.reshape(devices_all, N_BLK, TILE_SLOTS),
            group_ids,
            member_ids,
        ),
    )
    hidden = jnp.dot(aggregated.reshape(-1, FEAT), weight, precision=precise, preferred_element_type=jnp.float32)
    return jax.nn.relu(hidden + bias_vector[None, :])
```

```python
import functools

import jax
import jax.numpy as jnp
from jax import lax
from jax.experimental import pallas as pl
from jax.experimental.pallas import tpu as pltpu
from jax.sharding import PartitionSpec as P

MESH = pl.DeviceIdType.MESH
CUTS = (1, 2, 2, 1, 1, 1)
CHUNKS = len(CUTS)
PIECES = 4
PREPARES = 8
AHEAD = 2
LAUNCH_AT = 2


def column_sum(mask, values):
    return jnp.sum(jnp.where(mask, values, 0.0), axis=0, keepdims=True)


def halves(value):
    hi = value.astype(jnp.bfloat16)
    return hi, (value - hi.astype(jnp.float32)).astype(jnp.bfloat16)


def flat_row(ref, lanes):
    count, width = ref.shape
    spread = (
        lax.rem(lax.broadcasted_iota(jnp.int32, (width, lanes), 1), width)
        == lax.broadcasted_iota(jnp.int32, (width, lanes), 0)
    ).astype(jnp.float32)
    wide = jnp.dot(
        ref[...].astype(jnp.float32), spread,
        precision=lax.Precision.HIGHEST, preferred_element_type=jnp.float32,
    )
    mine = (
        lax.broadcasted_iota(jnp.int32, (count, lanes), 1) // width
        == lax.broadcasted_iota(jnp.int32, (count, lanes), 0)
    )
    return column_sum(mine, wide).astype(jnp.int32)


def kernel(cfg, x_hbm, ns_hbm, dest_hbm, src_hbm, w_hbm, b_hbm, a_hbm, o_hbm, *scratch):
    nb, ng, per, n_tiles, tile, feat, lanes = cfg
    chunks = CHUNKS
    widths = [feat * part // sum(CUTS) for part in CUTS]
    starts = [sum(widths[:c]) for c in range(chunks)]
    nz = nb // 2
    rows_local = ng * per
    sub = 8
    first = per * widths[0] // sub
    first_all = first + per // sub
    xs, sums, got = scratch[:chunks], scratch[chunks:2 * chunks], scratch[2 * chunks:3 * chunks]
    rest = scratch[3 * chunks:]
    (raw, at, part, total, flat, x_v, w_v, b_v, dest_v, src_v, ns_s, meta_v, meta_s, pick_v, pick_s,
     in_sem, raw_sem, meta_sem, out_sem, own_send, fwd_send, lane_recv, pair_recv, red_send, red_recv, ready) = rest

    g = lax.axis_index("grp")
    b = lax.axis_index("blk")
    z = b // 2
    core = b % 2
    pair = z * 2 + 1 - core
    middle = (z > 0) & (z < nz - 1)

    def onward(way):
        return z + 1 < nz if way == 0 else z >= 1

    def at_end(way):
        return z == 0 if way == 0 else z == nz - 1

    near = [g + 1 - 2 * lax.rem(g, 2), lax.rem(g + 2, ng)] if ng == 4 else [lax.rem(g + r, ng) for r in range(1, ng)]
    barrier = pltpu.get_barrier_semaphore()

    def greet(device):
        pl.semaphore_signal(barrier, inc=1, device_id=device, device_id_type=MESH)

    for way in range(2):
        @pl.when(onward(way))
        def _(way=way):
            greet((g, b + 2 if way == 0 else b - 2))
        if nz > 2:
            @pl.when(z == 2 if way == 0 else z == nz - 3)
            def _(way=way):
                greet((g, b - 4 if way == 0 else b + 4))
    greet((g, pair))
    for partner in near:
        greet((partner, b))
    heard = 1 + len(near) + sum(onward(way).astype(jnp.int32) for way in range(2))
    if nz > 2:
        heard = heard + sum(at_end(way).astype(jnp.int32) for way in range(2))

    loads = [
        pltpu.make_async_copy(src, dst, in_sem.at[i])
        for i, (src, dst) in enumerate(
            ((x_hbm, x_v), (w_hbm, w_v), (ns_hbm, ns_s), (dest_hbm, dest_v), (src_hbm, src_v), (b_hbm, b_v))
        )
    ]
    for copy in loads:
        copy.start()
    raws = [
        pltpu.make_async_copy(
            a_hbm.at[pl.ds(i * (n_tiles // nb), n_tiles // nb)],
            raw.at[pl.ds(i * (n_tiles // nb), n_tiles // nb)],
            raw_sem.at[i],
        )
        for i in range(nb)
    ]
    for copy in raws:
        copy.start()
    for copy in loads:
        copy.wait()

    w_hi, w_lo = halves(w_v[...])
    w_both = jnp.concatenate([w_hi, w_lo], axis=1)
    for j in range(per):
        hi, lo = halves(x_v[pl.ds(j * tile, tile), :])
        res = jnp.dot(
            jnp.concatenate([hi, lo], axis=0), w_both, preferred_element_type=jnp.float32
        )
        y = (res[:tile, :feat] + (res[:tile, feat:] + res[tile:, :feat])).T
        deep = widths[0] // sub
        flat[pl.ds(b * first_all + j * deep, deep)] = y[:widths[0], :].reshape(deep, sub, tile)
        for c in range(1, chunks):
            xs[c][b * per + j] = y[starts[c]:starts[c] + widths[c], :]
    row_id = lax.broadcasted_iota(jnp.int32, (per, tile), 0)
    slot_rows = jnp.zeros((per, tile), jnp.float32)
    for j in range(per):
        slot_rows = jnp.where(row_id == j, lax.rem(ns_s[j], nb * per).astype(jnp.float32), slot_rows)
    flat[pl.ds(b * first_all + first, per // sub)] = slot_rows.reshape(per // sub, sub, tile)

    iota_row = lax.broadcasted_iota(jnp.int32, (lanes, lanes), 1).astype(jnp.float32)
    iota_col = lax.broadcasted_iota(jnp.int32, (lanes, lanes), 0).astype(jnp.float32)
    dest = flat_row(dest_v, lanes)
    source = flat_row(src_v, lanes)
    rel = jnp.where(
        dest >= 0,
        lax.rem(dest // per - g + ng, ng) * per + lax.rem(jnp.maximum(dest, 0), per),
        rows_local,
    ).astype(jnp.float32)
    lane_id = lax.broadcasted_iota(jnp.int32, (1, lanes), 1)
    dest_b = jnp.broadcast_to(rel, (lanes, lanes))
    dest_t = dest_b.T
    before = (dest_t < dest_b) | ((dest_t == dest_b) & (iota_col < iota_row))
    rank = jnp.sum(before.astype(jnp.float32), axis=0, keepdims=True)
    rank_t = jnp.broadcast_to(rank, (lanes, lanes)).T
    hot = rank_t == iota_row
    order = column_sum(hot, iota_col)
    sorted_dest = column_sum(hot, dest_t)
    count_le = jnp.sum((dest_t <= iota_row).astype(jnp.float32), axis=0, keepdims=True)
    count_eq = jnp.sum((dest_t == iota_row).astype(jnp.float32), axis=0, keepdims=True)
    sorted_t = jnp.broadcast_to(sorted_dest, (lanes, lanes)).T
    previous = column_sum(iota_col == iota_row - 1.0, sorted_t)
    same = jnp.where((previous == sorted_dest) & (lane_id > 0), 1.0, 0.0)
    last = jnp.maximum(count_le - 1.0, 0.0)
    has = jnp.where(count_eq > 0.0, 1.0, 0.0)
    for i, row in enumerate((order, same, last, has)):
        meta_v[pl.ds(i, 1), :] = row.astype(jnp.int32)
    meta = pltpu.make_async_copy(meta_v, meta_s, meta_sem.at[0])
    meta.start()

    pl.semaphore_wait(barrier, heard)

    def rows(c, device):
        if c == 0:
            return flat.at[pl.ds(device * first_all, first_all)]
        return xs[c].at[pl.ds(device * per, per)]

    def send(c, device, target, s_sem, r_sem):
        return pltpu.make_async_remote_copy(
            rows(c, device), rows(c, device), s_sem, r_sem, device_id=(g, target), device_id_type=MESH
        )

    def own(c, way, steps=1):
        if way == 2:
            return send(c, b, pair, own_send.at[c, 4], pair_recv.at[c, z])
        hop = 2 * steps
        return send(c, b, b + hop if way == 0 else b - hop, own_send.at[c, 2 * steps - 2 + way], lane_recv.at[c, z])

    def forward(c, way, s, to_pair):
        origin = z - s if way == 0 else z + s
        device = origin * 2 + core
        if to_pair:
            return send(c, device, pair, fwd_send.at[c, way, s, 1], pair_recv.at[c, origin])
        return send(c, device, b + 2 if way == 0 else b - 2, fwd_send.at[c, way, s, 0], lane_recv.at[c, origin])

    def exists(way, s):
        return z - s >= 0 if way == 0 else z + s < nz

    def passes(way, s):
        go = exists(way, s) & onward(way)
        if s == 1 and nz > 2:
            go = go & (z != 1 if way == 0 else z != nz - 2)
        return go

    def launch(c):
        for way in range(2):
            @pl.when(onward(way))
            def _(way=way):
                own(c, way).start()
            if nz > 2:
                @pl.when(at_end(way))
                def _(way=way):
                    own(c, way, 2).start()
        own(c, 2).start()

    def service(c, s, who):
        for way in range(2):
            @pl.when(who & passes(way, s))
            def _(way=way):
                forward(c, way, s, False).wait_recv()
                forward(c, way, s, False).start()
                forward(c, way, s, True).start()
        for way in range(2):
            @pl.when(who & exists(way, s) & jnp.logical_not(passes(way, s)))
            def _(way=way):
                forward(c, way, s, False).wait_recv()
                forward(c, way, s, True).start()

    def entry(ref, row, i, size):
        return jnp.clip(ref[row, i], 0, size - 1)

    def reduce_copy(c, r):
        return pltpu.make_async_remote_copy(
            sums[c].at[r], got[c].at[r], red_send.at[c, r], red_recv.at[c, r],
            device_id=(lax.rem(g + r, ng), b), device_id_type=MESH,
        )

    def finish(c):
        for r in range(1, ng):
            reduce_copy(c, r).wait_recv()
        for j in range(per):
            acc = sums[c][0, j]
            for r in range(1, ng):
                acc = acc + got[c][r, j]
            total[j, pl.ds(starts[c], widths[c]), :] = acc

    def prepare(p, carry):
        hi, lo = halves(raw[entry(meta_s, 0, p, n_tiles)].T)
        at[p, :, pl.ds(0, tile)] = hi
        at[p, :, pl.ds(tile, tile)] = lo
        return carry

    def pick():
        for origin in range(nz):
            device = origin * 2 + 1 - core
            send(0, device, pair, own_send.at[0, 4], pair_recv.at[0, origin]).wait_recv()
        wanted = (lane_id // (n_tiles // nb)) * per + jnp.maximum(source, 0)
        slots = jnp.concatenate(
            [flat[pl.ds(device * first_all + first, per // sub)].reshape(per, tile) for device in range(nb)], axis=0
        )
        slots = jnp.concatenate([slots] * (lanes // tile), axis=1)
        position = lax.broadcasted_iota(jnp.int32, (nb * per, lanes), 0).astype(jnp.float32)
        place = jnp.minimum(column_sum(slots == wanted.astype(jnp.float32), position), nb * per - 1.0)
        place_t = jnp.broadcast_to(place, (lanes, lanes)).T
        picked = column_sum(hot, place_t).astype(jnp.int32)
        pick_v[pl.ds(0, 1), :] = picked
        pick_v[pl.ds(1, 1), :] = picked * (widths[0] // sub) + (picked // per) * (per // sub)
        copy = pltpu.make_async_copy(pick_v, pick_s, meta_sem.at[1])
        copy.start()
        copy.wait()

    def multiply_step(c, p, carry):
        fc = widths[c]
        if c == 0:
            row = entry(pick_s, 1, p, nb * first_all - fc // sub + 1)
            block = flat[pl.ds(row, fc // sub)].reshape(fc, tile)
        else:
            block = xs[c][entry(pick_s, 0, p, nb * per)]
        hi, lo = halves(block)
        both = jnp.concatenate([hi, lo], axis=0)
        res = jnp.dot(both, at[p], preferred_element_type=jnp.float32)
        out = res[:fc, :tile] + (res[:fc, tile:] + res[fc:, :tile])
        out = out + carry * meta_s[1, p].astype(jnp.float32)
        part[p, pl.ds(0, fc), :] = out
        return out

    for c in range(min(AHEAD, chunks)):
        launch(c)
    if ng == 4:
        pl.semaphore_signal(ready, inc=1, device_id=(lax.rem(g + 2, ng), b), device_id_type=MESH)

    def follow(c, s):
        service(c, s, middle)
        if s == min(LAUNCH_AT, nz - 2) and c + AHEAD < chunks:
            launch(c + AHEAD)

    meta.wait()
    for copy in raws:
        copy.wait()
    piece = n_tiles // PREPARES
    todo = list(range(1, nz - 1)) or [1]
    for q in range(PREPARES):
        lax.fori_loop(q * piece, (q + 1) * piece, prepare, 0, unroll=4)
        if q >= PREPARES // 2 - 1 and todo and q % 2:
            follow(0, todo.pop(0))
    while todo:
        follow(0, todo.pop(0))
    for s in range(1, nz):
        service(0, s, jnp.logical_not(middle))
    pick()

    piece = n_tiles // PIECES
    for c in range(chunks):
        fc = widths[c]
        if c:
            for origin in range(nz):
                device = origin * 2 + 1 - core
                send(c, device, pair, own_send.at[c, 4], pair_recv.at[c, origin]).wait_recv()
        todo = (list(range(1, nz - 1)) or [1]) if c + 1 < chunks else []

        def stretch(q, carry, c=c, todo=todo):
            for i in range(piece):
                carry = multiply_step(c, q * piece + i, carry)
            for k, s in enumerate(todo):
                @pl.when(q == min(k, PIECES - 1))
                def _(s=s):
                    follow(c + 1, s)
            return carry

        lax.fori_loop(0, PIECES, stretch, jnp.zeros((fc, tile), jnp.float32))
        if c == 0 and ng == 4:
            pl.semaphore_wait(ready, 1)
        for r in list(range(1, ng)) + [0]:
            for j in range(per):
                d = r * per + j
                sums[c][r, j] = part[entry(meta_s, 2, d, n_tiles), pl.ds(0, fc), :] * meta_s[3, d].astype(jnp.float32)
            if r:
                reduce_copy(c, r).start()
        if c + 1 < chunks:
            for s in range(1, nz):
                service(c + 1, s, jnp.logical_not(middle))

    for c in range(chunks):
        for way in range(2):
            @pl.when(onward(way))
            def _(c=c, way=way):
                own(c, way).wait_send()
            if nz > 2:
                @pl.when(at_end(way))
                def _(c=c, way=way):
                    own(c, way, 2).wait_send()
        own(c, 2).wait_send()
        for s in range(1, nz):
            for way in range(2):
                @pl.when(passes(way, s))
                def _(c=c, way=way, s=s):
                    forward(c, way, s, False).wait_send()
                @pl.when(exists(way, s))
                def _(c=c, way=way, s=s):
                    forward(c, way, s, True).wait_send()
    for c in range(chunks):
        finish(c)
    for j in range(per):
        x_v[pl.ds(j * tile, tile), :] = jnp.maximum(total[j].T + b_v[...], 0.0)
    out = pltpu.make_async_copy(x_v, o_hbm, out_sem)
    out.start()
    for c in range(chunks):
        for r in range(1, ng):
            reduce_copy(c, r).wait_send()
    out.wait()


def body(features, new_slot, tile_values, tile_dest, tile_source, weight, bias_vector):
    nb = lax.axis_size("blk")
    ng = lax.axis_size("grp")
    per = new_slot.shape[0]
    tile = tile_values.shape[-1]
    feat = features.shape[1]
    n_tiles = tile_dest.size
    lanes = n_tiles
    widths = [feat * part // sum(CUTS) for part in CUTS]
    nz = nb // 2
    cfg = (nb, ng, per, n_tiles, tile, feat, lanes)
    hbm = pl.BlockSpec(memory_space=pltpu.HBM)
    dma = pltpu.SemaphoreType.DMA
    local = tile_dest.shape[2:]
    return pl.pallas_call(
        functools.partial(kernel, cfg),
        out_shape=jax.ShapeDtypeStruct((per * tile, feat), jnp.float32),
        in_specs=[hbm] * 7,
        out_specs=hbm,
        scratch_shapes=[pltpu.VMEM((nb * per if c else 8, fc, tile), jnp.float32) for c, fc in enumerate(widths)]
        + [pltpu.VMEM((ng, per, fc, tile), jnp.float32) for fc in widths] * 2
        + [
            pltpu.VMEM((n_tiles, tile, tile), jnp.float32),
            pltpu.VMEM((n_tiles, tile, 2 * tile), jnp.bfloat16),
            pltpu.VMEM((n_tiles, max(widths), tile), jnp.float32),
            pltpu.VMEM((per, feat, tile), jnp.float32),
            pltpu.VMEM((nb * (per * widths[0] + per) // 8, 8, tile), jnp.float32),
            pltpu.VMEM((per * tile, feat), jnp.float32),
            pltpu.VMEM((feat, feat), jnp.float32),
            pltpu.VMEM((1, feat), jnp.float32),
            pltpu.VMEM(local, jnp.int32),
            pltpu.VMEM(local, jnp.int32),
            pltpu.SMEM((per,), jnp.int32),
            pltpu.VMEM((8, lanes), jnp.int32),
            pltpu.SMEM((8, lanes), jnp.int32),
            pltpu.VMEM((8, lanes), jnp.int32),
            pltpu.SMEM((8, lanes), jnp.int32),
            dma((6,)),
            dma((nb,)),
            dma((2,)),
            dma,
            dma((CHUNKS, 5)),
            dma((CHUNKS, 2, nz, 2)),
            dma((CHUNKS, nz)),
            dma((CHUNKS, nz)),
            dma((CHUNKS, ng)),
            dma((CHUNKS, ng)),
            pltpu.SemaphoreType.REGULAR,
        ],
        compiler_params=pltpu.CompilerParams(
            collective_id=0, has_side_effects=True, vmem_limit_bytes=63 << 20
        ),
    )(
        features,
        new_slot,
        tile_dest.reshape(local),
        tile_source.reshape(local),
        weight,
        bias_vector.reshape(1, feat),
        tile_values.reshape(n_tiles, tile, tile),
    )


def solution(mesh):
    return jax.shard_map(
        body,
        mesh=mesh,
        in_specs=(
            P(("grp", "blk"), None),
            P(("grp", "blk")),
            P("grp", "blk", None, None, None, None),
            P("grp", "blk", None, None),
            P("grp", "blk", None, None),
            P(),
            P(),
        ),
        out_specs=P(("grp", "blk"), None),
        check_vma=False,
    )
```

```python
import functools

import jax
import jax.numpy as jnp
from jax import lax
from jax.experimental import pallas as pl
from jax.experimental.pallas import tpu as pltpu
from jax.sharding import PartitionSpec as P

MESH = pl.DeviceIdType.MESH
CUTS = (1, 2, 2, 1, 1, 1)
CHUNKS = len(CUTS)
PIECES = 2
PREPARES = 8
AHEAD = 2
LAUNCH_AT = 2


def column_sum(mask, values):
    return jnp.sum(jnp.where(mask, values, 0.0), axis=0, keepdims=True)


def halves(value):
    hi = value.astype(jnp.bfloat16)
    return hi, (value - hi.astype(jnp.float32)).astype(jnp.bfloat16)


def flat_row(ref, lanes):
    count, width = ref.shape
    spread = (
        lax.rem(lax.broadcasted_iota(jnp.int32, (width, lanes), 1), width)
        == lax.broadcasted_iota(jnp.int32, (width, lanes), 0)
    ).astype(jnp.float32)
    wide = jnp.dot(
        ref[...].astype(jnp.float32), spread,
        precision=lax.Precision.HIGHEST, preferred_element_type=jnp.float32,
    )
    mine = (
        lax.broadcasted_iota(jnp.int32, (count, lanes), 1) // width
        == lax.broadcasted_iota(jnp.int32, (count, lanes), 0)
    )
    return column_sum(mine, wide).astype(jnp.int32)


def kernel(cfg, x_hbm, ns_hbm, dest_hbm, src_hbm, w_hbm, a_hbm, o_hbm, *scratch):
    nb, ng, per, n_tiles, tile, feat, lanes = cfg
    chunks = CHUNKS
    widths = [feat * part // sum(CUTS) for part in CUTS]
    starts = [sum(widths[:c]) for c in range(chunks)]
    nz = nb // 2
    rows_local = ng * per
    sub = 8
    first = per * widths[0] // sub
    first_all = first + per // sub
    xs, sums, got = scratch[:chunks], scratch[chunks:2 * chunks], scratch[2 * chunks:3 * chunks]
    total, rest = scratch[3 * chunks:4 * chunks], scratch[4 * chunks:]
    (raw, at, part, flat, x_v, w_v, dest_v, src_v, ns_s, meta_v, meta_s, pick_v, pick_s,
     in_sem, raw_sem, meta_sem, out_sem, own_send, fwd_send, lane_recv, pair_recv, red_send, red_recv, ready) = rest

    g = lax.axis_index("grp")
    b = lax.axis_index("blk")
    z = b // 2
    core = b % 2
    pair = z * 2 + 1 - core
    middle = (z > 0) & (z < nz - 1)

    def onward(way):
        return z + 1 < nz if way == 0 else z >= 1

    def at_end(way):
        return z == 0 if way == 0 else z == nz - 1

    near = [g + 1 - 2 * lax.rem(g, 2), lax.rem(g + 2, ng)] if ng == 4 else [lax.rem(g + r, ng) for r in range(1, ng)]
    barrier = pltpu.get_barrier_semaphore()

    def greet(device):
        pl.semaphore_signal(barrier, inc=1, device_id=device, device_id_type=MESH)

    for way in range(2):
        @pl.when(onward(way))
        def _(way=way):
            greet((g, b + 2 if way == 0 else b - 2))
        if nz > 2:
            @pl.when(z == 2 if way == 0 else z == nz - 3)
            def _(way=way):
                greet((g, b - 4 if way == 0 else b + 4))
    greet((g, pair))
    for partner in near:
        greet((partner, b))
    heard = 1 + len(near) + sum(onward(way).astype(jnp.int32) for way in range(2))
    if nz > 2:
        heard = heard + sum(at_end(way).astype(jnp.int32) for way in range(2))

    loads = [
        pltpu.make_async_copy(src, dst, in_sem.at[i])
        for i, (src, dst) in enumerate(
            ((x_hbm, x_v), (w_hbm, w_v), (ns_hbm, ns_s), (dest_hbm, dest_v), (src_hbm, src_v))
        )
    ]
    for copy in loads:
        copy.start()
    raws = [
        pltpu.make_async_copy(
            a_hbm.at[pl.ds(i * (n_tiles // nb), n_tiles // nb)],
            raw.at[pl.ds(i * (n_tiles // nb), n_tiles // nb)],
            raw_sem.at[i],
        )
        for i in range(nb)
    ]
    for copy in raws:
        copy.start()
    for copy in loads:
        copy.wait()

    w_hi, w_lo = halves(w_v[...])
    w_both = jnp.concatenate([w_hi, w_lo], axis=1)
    for j in range(per):
        hi, lo = halves(x_v[pl.ds(j * tile, tile), :])
        res = jnp.dot(
            jnp.concatenate([hi, lo], axis=0), w_both, preferred_element_type=jnp.float32
        )
        y = (res[:tile, :feat] + (res[:tile, feat:] + res[tile:, :feat])).T
        deep = widths[0] // sub
        flat[pl.ds(b * first_all + j * deep, deep)] = y[:widths[0], :].reshape(deep, sub, tile)
        for c in range(1, chunks):
            xs[c][b * per + j] = y[starts[c]:starts[c] + widths[c], :]
    row_id = lax.broadcasted_iota(jnp.int32, (per, tile), 0)
    slot_rows = jnp.zeros((per, tile), jnp.float32)
    for j in range(per):
        slot_rows = jnp.where(row_id == j, lax.rem(ns_s[j], nb * per).astype(jnp.float32), slot_rows)
    flat[pl.ds(b * first_all + first, per // sub)] = slot_rows.reshape(per // sub, sub, tile)

    pl.semaphore_wait(barrier, heard)

    def rows(c, device):
        if c == 0:
            return flat.at[pl.ds(device * first_all, first_all)]
        return xs[c].at[pl.ds(device * per, per)]

    def send(c, device, target, s_sem, r_sem):
        return pltpu.make_async_remote_copy(
            rows(c, device), rows(c, device), s_sem, r_sem, device_id=(g, target), device_id_type=MESH
        )

    def own(c, way, steps=1):
        if way == 2:
            return send(c, b, pair, own_send.at[c, 4], pair_recv.at[c, z])
        hop = 2 * steps
        return send(c, b, b + hop if way == 0 else b - hop, own_send.at[c, 2 * steps - 2 + way], lane_recv.at[c, z])

    def forward(c, way, s, to_pair):
        origin = z - s if way == 0 else z + s
        device = origin * 2 + core
        if to_pair:
            return send(c, device, pair, fwd_send.at[c, way, s, 1], pair_recv.at[c, origin])
        return send(c, device, b + 2 if way == 0 else b - 2, fwd_send.at[c, way, s, 0], lane_recv.at[c, origin])

    def exists(way, s):
        return z - s >= 0 if way == 0 else z + s < nz

    def passes(way, s):
        go = exists(way, s) & onward(way)
        if s == 1 and nz > 2:
            go = go & (z != 1 if way == 0 else z != nz - 2)
        return go

    def launch(c):
        for way in range(2):
            @pl.when(onward(way))
            def _(way=way):
                own(c, way).start()
            if nz > 2:
                @pl.when(at_end(way))
                def _(way=way):
                    own(c, way, 2).start()
        own(c, 2).start()

    def service(c, s, who):
        for way in range(2):
            @pl.when(who & passes(way, s))
            def _(way=way):
                forward(c, way, s, False).wait_recv()
                forward(c, way, s, False).start()
                forward(c, way, s, True).start()
        for way in range(2):
            @pl.when(who & exists(way, s) & jnp.logical_not(passes(way, s)))
            def _(way=way):
                forward(c, way, s, False).wait_recv()
                forward(c, way, s, True).start()

    def entry(ref, row, i, size):
        return jnp.clip(ref[row, i], 0, size - 1)

    def reduce_copy(c, r):
        return pltpu.make_async_remote_copy(
            sums[c].at[r], got[c].at[r], red_send.at[c, r], red_recv.at[c, r],
            device_id=(lax.rem(g + r, ng), b), device_id_type=MESH,
        )

    def result(c):
        return pltpu.make_async_copy(total[c], o_hbm.at[:, pl.ds(starts[c], widths[c]), :], out_sem.at[c])

    def finish(c):
        for r in range(1, ng):
            reduce_copy(c, r).wait_recv()
        for j in range(per):
            acc = sums[c][0, j]
            for r in range(1, ng):
                acc = acc + got[c][r, j]
            total[c][j] = acc
        result(c).start()

    def prepare(p, carry):
        hi, lo = halves(raw[entry(meta_s, 0, p, n_tiles)].T)
        at[p, :, pl.ds(0, tile)] = hi
        at[p, :, pl.ds(tile, tile)] = lo
        return carry

    def pick():
        for origin in range(nz):
            device = origin * 2 + 1 - core
            send(0, device, pair, own_send.at[0, 4], pair_recv.at[0, origin]).wait_recv()
        wanted = (lane_id // (n_tiles // nb)) * per + jnp.maximum(source, 0)
        slots = jnp.concatenate(
            [flat[pl.ds(device * first_all + first, per // sub)].reshape(per, tile) for device in range(nb)], axis=0
        )
        slots = jnp.concatenate([slots] * (lanes // tile), axis=1)
        position = lax.broadcasted_iota(jnp.int32, (nb * per, lanes), 0).astype(jnp.float32)
        place = jnp.minimum(column_sum(slots == wanted.astype(jnp.float32), position), nb * per - 1.0)
        place_t = jnp.broadcast_to(place, (lanes, lanes)).T
        picked = column_sum(hot, place_t).astype(jnp.int32)
        pick_v[pl.ds(0, 1), :] = picked
        pick_v[pl.ds(1, 1), :] = picked * (widths[0] // sub) + (picked // per) * (per // sub)
        copy = pltpu.make_async_copy(pick_v, pick_s, meta_sem.at[1])
        copy.start()
        copy.wait()

    def multiply_step(c, p, carry):
        fc = widths[c]
        if c == 0:
            row = entry(pick_s, 1, p, nb * first_all - fc // sub + 1)
            block = flat[pl.ds(row, fc // sub)].reshape(fc, tile)
        else:
            block = xs[c][entry(pick_s, 0, p, nb * per)]
        hi = block.astype(jnp.bfloat16).astype(jnp.float32)
        both = jnp.concatenate([hi, block - hi], axis=0).astype(jnp.bfloat16)
        res = jnp.dot(both, at[p], preferred_element_type=jnp.float32)
        out = res[:fc, :tile] + (res[:fc, tile:] + res[fc:, :tile])
        out = out + carry * meta_s[1, p].astype(jnp.float32)
        part[p, pl.ds(0, fc), :] = out
        return out

    launch(0)
    if ng == 4:
        pl.semaphore_signal(ready, inc=1, device_id=(lax.rem(g + 2, ng), b), device_id_type=MESH)

    iota_row = lax.broadcasted_iota(jnp.int32, (lanes, lanes), 1).astype(jnp.float32)
    iota_col = lax.broadcasted_iota(jnp.int32, (lanes, lanes), 0).astype(jnp.float32)
    dest = flat_row(dest_v, lanes)
    source = flat_row(src_v, lanes)
    rel = jnp.where(
        dest >= 0,
        lax.rem(dest // per - g + ng, ng) * per + lax.rem(jnp.maximum(dest, 0), per),
        rows_local,
    ).astype(jnp.float32)
    lane_id = lax.broadcasted_iota(jnp.int32, (1, lanes), 1)
    dest_b = jnp.broadcast_to(rel, (lanes, lanes))
    dest_t = dest_b.T
    before = (dest_t < dest_b) | ((dest_t == dest_b) & (iota_col < iota_row))
    rank = jnp.sum(before.astype(jnp.float32), axis=0, keepdims=True)
    rank_t = jnp.broadcast_to(rank, (lanes, lanes)).T
    hot = rank_t == iota_row
    order = column_sum(hot, iota_col)
    sorted_dest = column_sum(hot, dest_t)
    count_le = jnp.sum((dest_t <= iota_row).astype(jnp.float32), axis=0, keepdims=True)
    count_eq = jnp.sum((dest_t == iota_row).astype(jnp.float32), axis=0, keepdims=True)
    sorted_t = jnp.broadcast_to(sorted_dest, (lanes, lanes)).T
    previous = column_sum(iota_col == iota_row - 1.0, sorted_t)
    same = jnp.where((previous == sorted_dest) & (lane_id > 0), 1.0, 0.0)
    last = jnp.maximum(count_le - 1.0, 0.0)
    has = jnp.where(count_eq > 0.0, 1.0, 0.0)
    for i, row in enumerate((order, same, last, has)):
        meta_v[pl.ds(i, 1), :] = row.astype(jnp.int32)
    meta = pltpu.make_async_copy(meta_v, meta_s, meta_sem.at[0])
    meta.start()

    for c in range(1, min(AHEAD, chunks)):
        launch(c)

    def follow(c, s):
        service(c, s, middle)
        if s == min(LAUNCH_AT, nz - 2) and c + AHEAD < chunks:
            launch(c + AHEAD)

    meta.wait()
    for copy in raws:
        copy.wait()
    piece = n_tiles // PREPARES
    todo = list(range(1, nz - 1)) or [1]
    for q in range(PREPARES):
        lax.fori_loop(q * piece, (q + 1) * piece, prepare, 0, unroll=4)
        if q >= PREPARES // 2 - 1 and todo and q % 2:
            follow(0, todo.pop(0))
    while todo:
        follow(0, todo.pop(0))
    for s in range(1, nz):
        service(0, s, jnp.logical_not(middle))
    pick()

    piece = n_tiles // PIECES
    for c in range(chunks):
        fc = widths[c]
        if c:
            for origin in range(nz):
                device = origin * 2 + 1 - core
                send(c, device, pair, own_send.at[c, 4], pair_recv.at[c, origin]).wait_recv()
        todo = (list(range(1, nz - 1)) or [1]) if c + 1 < chunks else []

        def stretch(q, carry, c=c, todo=todo):
            for i in range(piece):
                carry = multiply_step(c, q * piece + i, carry)
            for k, s in enumerate(todo):
                @pl.when(q == min(k, PIECES - 1))
                def _(s=s):
                    follow(c + 1, s)
            return carry

        lax.fori_loop(0, PIECES, stretch, jnp.zeros((fc, tile), jnp.float32))
        if c == 0 and ng == 4:
            pl.semaphore_wait(ready, 1)
        for r in list(range(1, ng)) + [0]:
            for j in range(per):
                d = r * per + j
                sums[c][r, j] = part[entry(meta_s, 2, d, n_tiles), pl.ds(0, fc), :] * meta_s[3, d].astype(jnp.float32)
            if r:
                reduce_copy(c, r).start()
        if c + 1 < chunks:
            for s in range(1, nz):
                service(c + 1, s, jnp.logical_not(middle))

    for c in range(chunks):
        for way in range(2):
            @pl.when(onward(way))
            def _(c=c, way=way):
                own(c, way).wait_send()
            if nz > 2:
                @pl.when(at_end(way))
                def _(c=c, way=way):
                    own(c, way, 2).wait_send()
        own(c, 2).wait_send()
        for s in range(1, nz):
            for way in range(2):
                @pl.when(passes(way, s))
                def _(c=c, way=way, s=s):
                    forward(c, way, s, False).wait_send()
                @pl.when(exists(way, s))
                def _(c=c, way=way, s=s):
                    forward(c, way, s, True).wait_send()
    for c in range(chunks):
        finish(c)
    for c in range(chunks):
        for r in range(1, ng):
            reduce_copy(c, r).wait_send()
    for c in range(chunks):
        result(c).wait()


def body(features, new_slot, tile_values, tile_dest, tile_source, weight, bias_vector):
    nb = lax.axis_size("blk")
    ng = lax.axis_size("grp")
    per = new_slot.shape[0]
    tile = tile_values.shape[-1]
    feat = features.shape[1]
    n_tiles = tile_dest.size
    lanes = n_tiles
    widths = [feat * part // sum(CUTS) for part in CUTS]
    nz = nb // 2
    cfg = (nb, ng, per, n_tiles, tile, feat, lanes)
    hbm = pl.BlockSpec(memory_space=pltpu.HBM)
    dma = pltpu.SemaphoreType.DMA
    local = tile_dest.shape[2:]
    summed = pl.pallas_call(
        functools.partial(kernel, cfg),
        out_shape=jax.ShapeDtypeStruct((per, feat, tile), jnp.float32),
        in_specs=[hbm] * 6,
        out_specs=hbm,
        scratch_shapes=[pltpu.VMEM((nb * per if c else 8, fc, tile), jnp.float32) for c, fc in enumerate(widths)]
        + [pltpu.VMEM((ng, per, fc, tile), jnp.float32) for fc in widths] * 2
        + [pltpu.VMEM((per, fc, tile), jnp.float32) for fc in widths]
        + [
            pltpu.VMEM((n_tiles, tile, tile), jnp.float32),
            pltpu.VMEM((n_tiles, tile, 2 * tile), jnp.bfloat16),
            pltpu.VMEM((n_tiles, max(widths), tile), jnp.float32),
            pltpu.VMEM((nb * (per * widths[0] + per) // 8, 8, tile), jnp.float32),
            pltpu.VMEM((per * tile, feat), jnp.float32),
            pltpu.VMEM((feat, feat), jnp.float32),
            pltpu.VMEM(local, jnp.int32),
            pltpu.VMEM(local, jnp.int32),
            pltpu.SMEM((per,), jnp.int32),
            pltpu.VMEM((8, lanes), jnp.int32),
            pltpu.SMEM((8, lanes), jnp.int32),
            pltpu.VMEM((8, lanes), jnp.int32),
            pltpu.SMEM((8, lanes), jnp.int32),
            dma((5,)),
            dma((nb,)),
            dma((2,)),
            dma((CHUNKS,)),
            dma((CHUNKS, 5)),
            dma((CHUNKS, 2, nz, 2)),
            dma((CHUNKS, nz)),
            dma((CHUNKS, nz)),
            dma((CHUNKS, ng)),
            dma((CHUNKS, ng)),
            pltpu.SemaphoreType.REGULAR,
        ],
        compiler_params=pltpu.CompilerParams(
            collective_id=0, has_side_effects=True, vmem_limit_bytes=63 << 20
        ),
    )(
        features,
        new_slot,
        tile_dest.reshape(local),
        tile_source.reshape(local),
        weight,
        tile_values.reshape(n_tiles, tile, tile),
    )
    return jnp.maximum(summed.transpose(0, 2, 1).reshape(per * tile, feat) + bias_vector, 0.0)


def solution(mesh):
    return jax.shard_map(
        body,
        mesh=mesh,
        in_specs=(
            P(("grp", "blk"), None),
            P(("grp", "blk")),
            P("grp", "blk", None, None, None, None),
            P("grp", "blk", None, None),
            P("grp", "blk", None, None),
            P(),
            P(),
        ),
        out_specs=P(("grp", "blk"), None),
        check_vma=False,
    )
```

```python
import functools

import jax
import jax.numpy as jnp
from jax import lax
from jax.experimental import pallas as pl
from jax.experimental.pallas import tpu as pltpu
from jax.sharding import PartitionSpec as P

MESH = pl.DeviceIdType.MESH
CUTS = (1, 2, 2, 1, 1, 1)
CHUNKS = len(CUTS)
PIECES = 2
PREPARES = 8
AHEAD = 2
LAUNCH_AT = 2


def column_sum(mask, values):
    return jnp.sum(jnp.where(mask, values, 0.0), axis=0, keepdims=True)


def halves(value):
    hi = value.astype(jnp.bfloat16)
    return hi, (value - hi.astype(jnp.float32)).astype(jnp.bfloat16)


def flat_row(ref, lanes):
    count, width = ref.shape
    spread = (
        lax.rem(lax.broadcasted_iota(jnp.int32, (width, lanes), 1), width)
        == lax.broadcasted_iota(jnp.int32, (width, lanes), 0)
    ).astype(jnp.float32)
    wide = jnp.dot(
        ref[...].astype(jnp.float32), spread,
        precision=lax.Precision.HIGHEST, preferred_element_type=jnp.float32,
    )
    mine = (
        lax.broadcasted_iota(jnp.int32, (count, lanes), 1) // width
        == lax.broadcasted_iota(jnp.int32, (count, lanes), 0)
    )
    return column_sum(mine, wide).astype(jnp.int32)


def kernel(cfg, x_hbm, ns_hbm, dest_hbm, src_hbm, w_hbm, a_hbm, o_hbm, *scratch):
    nb, ng, per, n_tiles, tile, feat, lanes = cfg
    chunks = CHUNKS
    widths = [feat * part // sum(CUTS) for part in CUTS]
    starts = [sum(widths[:c]) for c in range(chunks)]
    nz = nb // 2
    rows_local = ng * per
    sub = 8
    first = per * widths[0] // sub
    first_all = first + per // sub
    xs, sums, got = scratch[:chunks], scratch[chunks:2 * chunks], scratch[2 * chunks:3 * chunks]
    total, rest = scratch[3 * chunks:4 * chunks], scratch[4 * chunks:]
    (raw, at, part, flat, x_v, w_v, dest_v, src_v, ns_s, meta_v, meta_s, pick_v, pick_s,
     in_sem, raw_sem, meta_sem, out_sem, own_send, fwd_send, lane_recv, pair_recv, red_send, red_recv, ready) = rest

    g = lax.axis_index("grp")
    b = lax.axis_index("blk")
    z = b // 2
    core = b % 2
    pair = z * 2 + 1 - core
    middle = (z > 0) & (z < nz - 1)

    def onward(way):
        return z + 1 < nz if way == 0 else z >= 1

    def at_end(way):
        return z == 0 if way == 0 else z == nz - 1

    near = [g + 1 - 2 * lax.rem(g, 2), lax.rem(g + 2, ng)] if ng == 4 else [lax.rem(g + r, ng) for r in range(1, ng)]
    barrier = pltpu.get_barrier_semaphore()

    def greet(device):
        pl.semaphore_signal(barrier, inc=1, device_id=device, device_id_type=MESH)

    for way in range(2):
        @pl.when(onward(way))
        def _(way=way):
            greet((g, b + 2 if way == 0 else b - 2))
        if nz > 2:
            @pl.when(z == 2 if way == 0 else z == nz - 3)
            def _(way=way):
                greet((g, b - 4 if way == 0 else b + 4))
    greet((g, pair))
    for partner in near:
        greet((partner, b))
    heard = 1 + len(near) + sum(onward(way).astype(jnp.int32) for way in range(2))
    if nz > 2:
        heard = heard + sum(at_end(way).astype(jnp.int32) for way in range(2))

    loads = [
        pltpu.make_async_copy(src, dst, in_sem.at[i])
        for i, (src, dst) in enumerate(
            [(w_hbm, w_v)]
            + [(x_hbm.at[pl.ds(j * tile, tile)], x_v.at[pl.ds(j * tile, tile)]) for j in range(per)]
            + [(ns_hbm, ns_s), (dest_hbm, dest_v), (src_hbm, src_v)]
        )
    ]
    for copy in loads:
        copy.start()
    raws = [
        pltpu.make_async_copy(
            a_hbm.at[pl.ds(i * (n_tiles // nb), n_tiles // nb)],
            raw.at[pl.ds(i * (n_tiles // nb), n_tiles // nb)],
            raw_sem.at[i],
        )
        for i in range(nb)
    ]
    for copy in raws:
        copy.start()
    loads[0].wait()
    w_hi, w_lo = halves(w_v[...])
    w_both = jnp.concatenate([w_hi, w_lo], axis=1)
    for j in range(per):
        loads[1 + j].wait()
        hi, lo = halves(x_v[pl.ds(j * tile, tile), :])
        res = jnp.dot(
            jnp.concatenate([hi, lo], axis=0), w_both, preferred_element_type=jnp.float32
        )
        y = (res[:tile, :feat] + (res[:tile, feat:] + res[tile:, :feat])).T
        deep = widths[0] // sub
        flat[pl.ds(b * first_all + j * deep, deep)] = y[:widths[0], :].reshape(deep, sub, tile)
        for c in range(1, chunks):
            xs[c][b * per + j] = y[starts[c]:starts[c] + widths[c], :]
    loads[1 + per].wait()
    row_id = lax.broadcasted_iota(jnp.int32, (per, tile), 0)
    slot_rows = jnp.zeros((per, tile), jnp.float32)
    for j in range(per):
        slot_rows = jnp.where(row_id == j, lax.rem(ns_s[j], nb * per).astype(jnp.float32), slot_rows)
    flat[pl.ds(b * first_all + first, per // sub)] = slot_rows.reshape(per // sub, sub, tile)

    pl.semaphore_wait(barrier, heard)

    def rows(c, device):
        if c == 0:
            return flat.at[pl.ds(device * first_all, first_all)]
        return xs[c].at[pl.ds(device * per, per)]

    def send(c, device, target, s_sem, r_sem):
        return pltpu.make_async_remote_copy(
            rows(c, device), rows(c, device), s_sem, r_sem, device_id=(g, target), device_id_type=MESH
        )

    def own(c, way, steps=1):
        if way == 2:
            return send(c, b, pair, own_send.at[c, 4], pair_recv.at[c, z])
        hop = 2 * steps
        return send(c, b, b + hop if way == 0 else b - hop, own_send.at[c, 2 * steps - 2 + way], lane_recv.at[c, z])

    def forward(c, way, s, to_pair):
        origin = z - s if way == 0 else z + s
        device = origin * 2 + core
        if to_pair:
            return send(c, device, pair, fwd_send.at[c, way, s, 1], pair_recv.at[c, origin])
        return send(c, device, b + 2 if way == 0 else b - 2, fwd_send.at[c, way, s, 0], lane_recv.at[c, origin])

    def exists(way, s):
        return z - s >= 0 if way == 0 else z + s < nz

    def passes(way, s):
        go = exists(way, s) & onward(way)
        if s == 1 and nz > 2:
            go = go & (z != 1 if way == 0 else z != nz - 2)
        return go

    def launch(c):
        @pl.when(onward(1) & (z < nz // 2))
        def _():
            own(c, 1).start()
        for way in range(2):
            @pl.when(onward(way) & ((way == 0) | (z >= nz // 2)))
            def _(way=way):
                own(c, way).start()
            if nz > 2:
                @pl.when(at_end(way))
                def _(way=way):
                    own(c, way, 2).start()
        own(c, 2).start()

    def service(c, s, who):
        for way in range(2):
            @pl.when(who & passes(way, s))
            def _(way=way):
                forward(c, way, s, False).wait_recv()
                forward(c, way, s, False).start()
                forward(c, way, s, True).start()
        for way in range(2):
            @pl.when(who & exists(way, s) & jnp.logical_not(passes(way, s)))
            def _(way=way):
                forward(c, way, s, False).wait_recv()
                forward(c, way, s, True).start()

    def entry(ref, row, i, size):
        return jnp.clip(ref[row, i], 0, size - 1)

    def reduce_copy(c, r):
        return pltpu.make_async_remote_copy(
            sums[c].at[r], got[c].at[r], red_send.at[c, r], red_recv.at[c, r],
            device_id=(lax.rem(g + r, ng), b), device_id_type=MESH,
        )

    def result(c):
        return pltpu.make_async_copy(total[c], o_hbm.at[:, pl.ds(starts[c], widths[c]), :], out_sem.at[c])

    def finish(c):
        for r in range(1, ng):
            reduce_copy(c, r).wait_recv()
        for j in range(per):
            acc = sums[c][0, j]
            for r in range(1, ng):
                acc = acc + got[c][r, j]
            total[c][j] = acc
        result(c).start()

    def prepare(p, carry):
        hi, lo = halves(raw[entry(meta_s, 0, p, n_tiles)].T)
        at[p, :, pl.ds(0, tile)] = hi
        at[p, :, pl.ds(tile, tile)] = lo
        return carry

    def pick():
        for origin in range(nz):
            device = origin * 2 + 1 - core
            send(0, device, pair, own_send.at[0, 4], pair_recv.at[0, origin]).wait_recv()
        wanted = (lane_id // (n_tiles // nb)) * per + jnp.maximum(source, 0)
        slots = jnp.concatenate(
            [flat[pl.ds(device * first_all + first, per // sub)].reshape(per, tile) for device in range(nb)], axis=0
        )
        slots = jnp.concatenate([slots] * (lanes // tile), axis=1)
        position = lax.broadcasted_iota(jnp.int32, (nb * per, lanes), 0).astype(jnp.float32)
        place = jnp.minimum(column_sum(slots == wanted.astype(jnp.float32), position), nb * per - 1.0)
        place_t = jnp.broadcast_to(place, (lanes, lanes)).T
        picked = column_sum(hot, place_t).astype(jnp.int32)
        pick_v[pl.ds(0, 1), :] = picked
        pick_v[pl.ds(1, 1), :] = picked * (widths[0] // sub) + (picked // per) * (per // sub)
        copy = pltpu.make_async_copy(pick_v, pick_s, meta_sem.at[1])
        copy.start()
        copy.wait()

    def multiply_step(c, p, carry):
        fc = widths[c]
        if c == 0:
            row = entry(pick_s, 1, p, nb * first_all - fc // sub + 1)
            block = flat[pl.ds(row, fc // sub)].reshape(fc, tile)
        else:
            block = xs[c][entry(pick_s, 0, p, nb * per)]
        hi = block.astype(jnp.bfloat16).astype(jnp.float32)
        both = jnp.concatenate([hi, block - hi], axis=0).astype(jnp.bfloat16)
        res = jnp.dot(both, at[p], preferred_element_type=jnp.float32)
        out = res[:fc, :tile] + (res[:fc, tile:] + res[fc:, :tile])
        out = out + carry * meta_s[1, p].astype(jnp.float32)
        part[p, pl.ds(0, fc), :] = out
        return out

    launch(0)
    if ng == 4:
        pl.semaphore_signal(ready, inc=1, device_id=(lax.rem(g + 2, ng), b), device_id_type=MESH)

    iota_row = lax.broadcasted_iota(jnp.int32, (lanes, lanes), 1).astype(jnp.float32)
    iota_col = lax.broadcasted_iota(jnp.int32, (lanes, lanes), 0).astype(jnp.float32)
    for copy in loads[2 + per:]:
        copy.wait()
    dest = flat_row(dest_v, lanes)
    source = flat_row(src_v, lanes)
    rel = jnp.where(
        dest >= 0,
        lax.rem(dest // per - g + ng, ng) * per + lax.rem(jnp.maximum(dest, 0), per),
        rows_local,
    ).astype(jnp.float32)
    lane_id = lax.broadcasted_iota(jnp.int32, (1, lanes), 1)
    dest_b = jnp.broadcast_to(rel, (lanes, lanes))
    dest_t = dest_b.T
    before = (dest_t < dest_b) | ((dest_t == dest_b) & (iota_col < iota_row))
    rank = jnp.sum(before.astype(jnp.float32), axis=0, keepdims=True)
    rank_t = jnp.broadcast_to(rank, (lanes, lanes)).T
    hot = rank_t == iota_row
    order = column_sum(hot, iota_col)
    sorted_dest = column_sum(hot, dest_t)
    count_le = jnp.sum((dest_t <= iota_row).astype(jnp.float32), axis=0, keepdims=True)
    count_eq = jnp.sum((dest_t == iota_row).astype(jnp.float32), axis=0, keepdims=True)
    sorted_t = jnp.broadcast_to(sorted_dest, (lanes, lanes)).T
    previous = column_sum(iota_col == iota_row - 1.0, sorted_t)
    same = jnp.where((previous == sorted_dest) & (lane_id > 0), 1.0, 0.0)
    last = jnp.maximum(count_le - 1.0, 0.0)
    has = jnp.where(count_eq > 0.0, 1.0, 0.0)
    for i, row in enumerate((order, same, last, has)):
        meta_v[pl.ds(i, 1), :] = row.astype(jnp.int32)
    meta = pltpu.make_async_copy(meta_v, meta_s, meta_sem.at[0])
    meta.start()

    for c in range(1, min(AHEAD, chunks)):
        launch(c)

    def follow(c, s):
        service(c, s, middle)
        if s == min(LAUNCH_AT if c else 1, nz - 2) and c + AHEAD < chunks:
            launch(c + AHEAD)

    meta.wait()
    for copy in raws:
        copy.wait()
    piece = n_tiles // PREPARES
    todo = list(range(1, nz - 1)) or [1]
    for q in range(PREPARES):
        lax.fori_loop(q * piece, (q + 1) * piece, prepare, 0, unroll=4)
        if q >= PREPARES // 2 - 1 and todo and q % 2:
            follow(0, todo.pop(0))
    while todo:
        follow(0, todo.pop(0))
    for s in range(1, nz):
        service(0, s, jnp.logical_not(middle))
    pick()

    piece = n_tiles // PIECES
    for c in range(chunks):
        fc = widths[c]
        if c:
            for origin in range(nz):
                device = origin * 2 + 1 - core
                send(c, device, pair, own_send.at[c, 4], pair_recv.at[c, origin]).wait_recv()
        todo = (list(range(1, nz - 1)) or [1]) if c + 1 < chunks else []

        def stretch(q, carry, c=c, todo=todo):
            for i in range(piece):
                carry = multiply_step(c, q * piece + i, carry)
            for k, s in enumerate(todo):
                @pl.when(q == min(k, PIECES - 1))
                def _(s=s):
                    follow(c + 1, s)
            return carry

        lax.fori_loop(0, PIECES, stretch, jnp.zeros((fc, tile), jnp.float32))
        if c == 0 and ng == 4:
            pl.semaphore_wait(ready, 1)
        for r in list(range(1, ng)) + [0]:
            for j in range(per):
                d = r * per + j
                sums[c][r, j] = part[entry(meta_s, 2, d, n_tiles), pl.ds(0, fc), :] * meta_s[3, d].astype(jnp.float32)
            if r:
                reduce_copy(c, r).start()
        if c + 1 < chunks:
            for s in range(1, nz):
                service(c + 1, s, jnp.logical_not(middle))

    for c in range(chunks):
        for way in range(2):
            @pl.when(onward(way))
            def _(c=c, way=way):
                own(c, way).wait_send()
            if nz > 2:
                @pl.when(at_end(way))
                def _(c=c, way=way):
                    own(c, way, 2).wait_send()
        own(c, 2).wait_send()
        for s in range(1, nz):
            for way in range(2):
                @pl.when(passes(way, s))
                def _(c=c, way=way, s=s):
                    forward(c, way, s, False).wait_send()
                @pl.when(exists(way, s))
                def _(c=c, way=way, s=s):
                    forward(c, way, s, True).wait_send()
    for c in range(chunks):
        finish(c)
    for c in range(chunks):
        for r in range(1, ng):
            reduce_copy(c, r).wait_send()
    for c in range(chunks):
        result(c).wait()


def body(features, new_slot, tile_values, tile_dest, tile_source, weight, bias_vector):
    nb = lax.axis_size("blk")
    ng = lax.axis_size("grp")
    per = new_slot.shape[0]
    tile = tile_values.shape[-1]
    feat = features.shape[1]
    n_tiles = tile_dest.size
    lanes = n_tiles
    widths = [feat * part // sum(CUTS) for part in CUTS]
    nz = nb // 2
    cfg = (nb, ng, per, n_tiles, tile, feat, lanes)
    hbm = pl.BlockSpec(memory_space=pltpu.HBM)
    dma = pltpu.SemaphoreType.DMA
    local = tile_dest.shape[2:]
    summed = pl.pallas_call(
        functools.partial(kernel, cfg),
        out_shape=jax.ShapeDtypeStruct((per, feat, tile), jnp.float32),
        in_specs=[hbm] * 6,
        out_specs=hbm,
        scratch_shapes=[pltpu.VMEM((nb * per if c else 8, fc, tile), jnp.float32) for c, fc in enumerate(widths)]
        + [pltpu.VMEM((ng, per, fc, tile), jnp.float32) for fc in widths] * 2
        + [pltpu.VMEM((per, fc, tile), jnp.float32) for fc in widths]
        + [
            pltpu.VMEM((n_tiles, tile, tile), jnp.float32),
            pltpu.VMEM((n_tiles, tile, 2 * tile), jnp.bfloat16),
            pltpu.VMEM((n_tiles, max(widths), tile), jnp.float32),
            pltpu.VMEM((nb * (per * widths[0] + per) // 8, 8, tile), jnp.float32),
            pltpu.VMEM((per * tile, feat), jnp.float32),
            pltpu.VMEM((feat, feat), jnp.float32),
            pltpu.VMEM(local, jnp.int32),
            pltpu.VMEM(local, jnp.int32),
            pltpu.SMEM((per,), jnp.int32),
            pltpu.VMEM((8, lanes), jnp.int32),
            pltpu.SMEM((8, lanes), jnp.int32),
            pltpu.VMEM((8, lanes), jnp.int32),
            pltpu.SMEM((8, lanes), jnp.int32),
            dma((4 + per,)),
            dma((nb,)),
            dma((2,)),
            dma((CHUNKS,)),
            dma((CHUNKS, 5)),
            dma((CHUNKS, 2, nz, 2)),
            dma((CHUNKS, nz)),
            dma((CHUNKS, nz)),
            dma((CHUNKS, ng)),
            dma((CHUNKS, ng)),
            pltpu.SemaphoreType.REGULAR,
        ],
        compiler_params=pltpu.CompilerParams(
            collective_id=0, has_side_effects=True, vmem_limit_bytes=63 << 20
        ),
    )(
        features,
        new_slot,
        tile_dest.reshape(local),
        tile_source.reshape(local),
        weight,
        tile_values.reshape(n_tiles, tile, tile),
    )
    return jnp.maximum(summed.transpose(0, 2, 1).reshape(per * tile, feat) + bias_vector, 0.0)


def solution(mesh):
    return jax.shard_map(
        body,
        mesh=mesh,
        in_specs=(
            P(("grp", "blk"), None),
            P(("grp", "blk")),
            P("grp", "blk", None, None, None, None),
            P("grp", "blk", None, None),
            P("grp", "blk", None, None),
            P(),
            P(),
        ),
        out_specs=P(("grp", "blk"), None),
        check_vma=False,
    )
```
